512 devices in a mesh: wide: 8 (over y), row: 64 (over z, x, core).
Axes of the slice: x: 4, y: 8, z: 8, core: 2. Of those that a mesh axis runs over, the one named last changes fastest.
Arguments:
- columns: float32 [16384, 2048], P('row', 'wide'), may hold values from -40 to 40, as said below
Outputs:
- rotated: float32 [16384, 2048], P('row', 'wide')
The draws below stay inside these ranges and needn't reach their ends.
Inputs may be any that keep to these rules, and one draw needn't show every extreme that they name: `columns`: columns have differing scales.
All inputs are finite; a program needn't handle non-finite values.
Results may differ from the reference program's by a relative error of at most 0.00021.
Values sent between devices are 32-bit elements; how exact they have to be, the bound alone decides.
A program may use at most 64 MiB of HBM per device.

```python
import jax
import jax.numpy as jnp
from jax import lax

M = 16384
BLOCK = 128
ROUNDS = 4
N_WIDE = 8


def draw_columns(key, part):
    first_key, second_key = jax.random.split(key, 2)
    column_count = 2 * BLOCK * N_WIDE
    scales = jnp.exp(jax.random.uniform(first_key, (column_count,), jnp.float32, 0.0, jnp.log(4.0)))
    entries = jnp.clip(jax.random.normal(second_key, (M, column_count), jnp.float32), -6.0, 6.0)
    return entries * scales[None, :]


def setup_inputs(seed: int = 0) -> dict:
    arg_keys = jax.random.split(jax.random.key(seed), 2)
    return {
        "columns": draw_columns(jax.random.fold_in(arg_keys[1], 71), 0),
    }


def rotation(gram_matrix):
    width_count = gram_matrix.shape[0]
    positions = jnp.arange(width_count)
    signs = jnp.where(positions[:, None] < positions[None, :], 1.0, -1.0).astype(jnp.float32)
    column_norms = jnp.diagonal(gram_matrix)
    off_diagonal = gram_matrix - jnp.diag(column_norms)
    generator = signs * off_diagonal / (column_norms[:, None] + column_norms[None, :] + 1e-06)
    identity = jnp.eye(width_count, dtype=jnp.float32)
    cayley_half = identity + 0.5 * generator
    normal_matrix = jnp.dot(cayley_half.T, cayley_half, precision=lax.Precision.HIGHEST)
    lower_factor = jnp.linalg.cholesky(normal_matrix)
    partial_solve = lax.linalg.triangular_solve(lower_factor, cayley_half, left_side=True, lower=True)
    solved = lax.linalg.triangular_solve(lower_factor, partial_solve, left_side=True, lower=True, transpose_a=True)
    return jnp.dot(cayley_half, solved, precision=lax.Precision.HIGHEST)

def rotate_pair(pair_parts):
    upper_block, lower_block = pair_parts
    paired = jnp.concatenate([upper_block, lower_block], axis=1)
    gram_matrix = jnp.dot(paired.T, paired, precision=lax.Precision.HIGHEST)
    turned = jnp.dot(paired, rotation(gram_matrix), precision=lax.Precision.HIGHEST)
    return (turned[:, :BLOCK], turned[:, BLOCK:])

def reference(columns):
    blocks = columns.reshape(M, N_WIDE, 2, BLOCK).transpose(1, 2, 0, 3)
    uppers = blocks[:, 0]
    lowers = blocks[:, 1]
    for rounds_done in range(ROUNDS):
        if rounds_done > 0:
            lowers = jnp.roll(lowers, 1, axis=0)
        uppers, lowers = lax.map(rotate_pair, (uppers, lowers))
    lowers = jnp.roll(lowers, -(ROUNDS - 1), axis=0)
    stacked = jnp.stack([uppers, lowers], axis=1)
    return stacked.transpose(2, 0, 1, 3).reshape(M, 2 * BLOCK * N_WIDE)
```

```python
import functools

import jax
import jax.numpy as jnp
from jax import lax
from jax.experimental import pallas as pl
from jax.experimental.pallas import tpu as pltpu
from jax.sharding import PartitionSpec as P

ROUNDS = 4
BLOCK = 128
MESH = pl.DeviceIdType.MESH
F32 = jnp.float32
BF16 = jnp.bfloat16
SERIES_TOL = 1e-7
NEWTON_STEPS = 17


def dims(trans_a, trans_b):
    return (((0 if trans_a else 1,), (1 if trans_b else 0,)), ((), ()))


def dot1(a, b, trans_a=False):
    return lax.dot_general(a.astype(BF16), b.astype(BF16), dims(trans_a, False), preferred_element_type=F32)


def split(x):
    high = x.astype(BF16)
    return high, (x - high.astype(F32)).astype(BF16)


def dot3(a, b, trans_a=False):
    a_high, a_low = split(a)
    b_high, b_low = split(b)
    d = functools.partial(lax.dot_general, dimension_numbers=dims(trans_a, False), preferred_element_type=F32)
    return d(a_high, b_high) + (d(a_high, b_low) + d(a_low, b_high))


def dot6(a, b):
    return lax.dot_general(a, b, dims(False, False), precision=lax.Precision.HIGHEST, preferred_element_type=F32)


def iotas(shape):
    return lax.broadcasted_iota(jnp.int32, shape, 0), lax.broadcasted_iota(jnp.int32, shape, 1)


def half_generator(uu, ul, ll):
    rows, cols = iotas((BLOCK, BLOCK))
    eye = rows == cols
    half_sign = jnp.where(rows < cols, 0.5, jnp.where(rows > cols, -0.5, 0.0)).astype(F32)

    def norms(block):
        only = jnp.where(eye, block, 0.0)
        return jnp.sum(only, axis=1, keepdims=True), jnp.sum(only, axis=0, keepdims=True)

    u_col, u_row = norms(uu)
    l_col, l_row = norms(ll)
    a_uu = half_sign * uu / (u_col + u_row + 1e-06)
    a_ll = half_sign * ll / (l_col + l_row + 1e-06)
    a_ul = 0.5 * ul / (u_col + l_row + 1e-06)
    top = jnp.concatenate([a_uu, a_ul], axis=1)
    low = jnp.concatenate([-a_ul.T, a_ll], axis=1)
    return jnp.concatenate([top, low], axis=0)


def series_turn(a):
    a2 = dot3(a, a)
    both = dot1(jnp.concatenate([a, a2], axis=0), a2)
    width = a.shape[0]
    a3, a4 = both[:width], both[width:]
    first = a + a2 + a3
    turn = 2.0 * (first + (a4 + dot1(first, a4)))
    return turn, jnp.sum(a4 * a4, keepdims=True)


def newton_turn(a, scratch):
    width = a.shape[0]
    rows, cols = iotas((width, width))
    eye = (rows == cols).astype(F32)
    a2 = dot6(a, a)
    bound = jnp.max(jnp.sum(jnp.abs(a2), axis=1, keepdims=True), axis=0, keepdims=True)
    scratch[0] = eye - a
    scratch[1] = (eye + a) * (2.0 / (2.0 + bound))

    def step(_, carry):
        x = scratch[1]
        residual = (rows == cols).astype(F32) - dot6(scratch[0], x)
        scratch[1] = x + dot6(x, residual)
        return carry

    lax.fori_loop(0, NEWTON_STEPS, step, 0)
    return 2.0 * (scratch[1] - eye)


def kernel(n_wide, n_near, n_far, series, x_ref, out_ref, flag_ref,
           sent0, near0, far0, whole0, sent, near, far, whole,
           low_out, low_in, gram_out, gram_in, last_out, last_in, flag_out, flags, newton,
           send_sem, recv_sem, shift_send, shift_recv, last_send, last_recv, flag_send, flag_recv):
    wide, row = lax.axis_index("wide"), lax.axis_index("row")
    me_near, me_far = lax.rem(row, n_near), lax.div(row, n_near)

    def near_peer(k):
        other = lax.rem(me_near + k, n_near)
        return other, {"row": me_far * n_near + other}

    def far_peer(k):
        return {"row": lax.rem(me_far + k, n_far) * n_near + me_near}

    def wide_peer(k):
        return {"wide": lax.rem(wide + (k + n_wide), n_wide)}

    barrier = pltpu.get_barrier_semaphore()
    for k in range(1, n_near):
        pl.semaphore_signal(barrier, inc=1, device_id=near_peer(k)[1], device_id_type=MESH)
    for k in range(1, n_far):
        pl.semaphore_signal(barrier, inc=1, device_id=far_peer(k), device_id_type=MESH)
    for k in range(1, n_wide):
        pl.semaphore_signal(barrier, inc=1, device_id=wide_peer(k), device_id_type=MESH)

    sends = []

    def send(src, dst, ssem, rsem, peer):
        copy = pltpu.make_async_remote_copy(
            src_ref=src, dst_ref=dst, send_sem=ssem, recv_sem=rsem, device_id=peer, device_id_type=MESH
        )
        copy.start()
        sends.append(copy)
        return copy

    def reduce_rows(r, out, near_buf, far_buf, whole_buf):
        copies = []
        for k in range(1, n_near):
            other, peer = near_peer(k)
            copies.append(send(out.at[other], near_buf.at[me_near], send_sem.at[r, 0, k], recv_sem.at[r, 0, k], peer))
        near_buf[me_near] = out[me_near]
        for copy in copies:
            copy.wait_recv()
        total = near_buf[0]
        for i in range(1, n_near):
            total = total + near_buf[i]
        far_buf[me_far] = total
        copies = [
            send(far_buf.at[me_far], far_buf.at[me_far], send_sem.at[r, 1, k], recv_sem.at[r, 1, k], far_peer(k))
            for k in range(1, n_far)
        ]
        for copy in copies:
            copy.wait_recv()
        total = far_buf[0]
        for i in range(1, n_far):
            total = total + far_buf[i]
        whole_buf[me_near] = total
        copies = [
            send(whole_buf.at[me_near], whole_buf.at[me_near], send_sem.at[r, 2, k], recv_sem.at[r, 2, k],
                 near_peer(k)[1])
            for k in range(1, n_near)
        ]
        return copies

    upper, lower = x_ref[:, :BLOCK], x_ref[:, BLOCK:]
    local = dot3(jnp.concatenate([upper, lower], axis=1), jnp.concatenate([upper, lower], axis=1), True)
    payload = jnp.concatenate([local[:BLOCK, BLOCK:], local[:BLOCK, :BLOCK], local[BLOCK:, BLOCK:]], axis=0)
    sent0[...] = payload.reshape(sent0.shape)
    pl.semaphore_wait(barrier, (n_near - 1) + (n_far - 1) + (n_wide - 1))

    worst = jnp.zeros((1, 1), F32)
    for r in range(ROUNDS):
        if r == 0:
            copies = reduce_rows(0, sent0, near0, far0, whole0)
            for copy in copies:
                copy.wait_recv()
            gram = whole0[...].reshape(3 * BLOCK, BLOCK)
            ul, uu, ll = gram[:BLOCK], gram[BLOCK:2 * BLOCK], gram[2 * BLOCK:]
        else:
            copies = reduce_rows(r, sent.at[r - 1], near.at[r - 1], far.at[r - 1], whole.at[r - 1])
            for copy in copies:
                copy.wait_recv()
            gram_copy.wait_recv()
            ul = whole[r - 1].reshape(BLOCK, BLOCK)
            uu, ll = kept_uu, gram_in[r - 1]
        a = half_generator(uu, ul, ll)
        if series:
            turn, rest = series_turn(a)
            worst = jnp.maximum(worst, rest)
        else:
            turn = newton_turn(a, newton)
        pair = jnp.concatenate([upper, lower], axis=1)
        turned = pair + dot3(pair, turn)
        upper = turned[:, :BLOCK]
        if r == ROUNDS - 1:
            last_out[...] = turned[:, BLOCK:]
            last = send(last_out, last_in, last_send, last_recv, wide_peer(-(ROUNDS - 1)))
            out_ref[:, :BLOCK] = upper
            break
        low_out[r] = turned[:, BLOCK:]
        low_copy = send(low_out.at[r], low_in.at[r], shift_send.at[r, 0], shift_recv.at[r, 0], wide_peer(1))
        full = jnp.concatenate(
            [jnp.concatenate([uu, ul], axis=1), jnp.concatenate([ul.T, ll], axis=1)], axis=0
        )
        half = full + dot3(full, turn)
        left, right = half[:, :BLOCK], half[:, BLOCK:]
        kept_uu = left[:BLOCK] + dot3(turn[:, :BLOCK], left, True)
        gram_out[r] = right[BLOCK:] + dot3(turn[:, BLOCK:], right, True)
        gram_copy = send(gram_out.at[r], gram_in.at[r], shift_send.at[r, 1], shift_recv.at[r, 1], wide_peer(1))
        low_copy.wait_recv()
        lower = low_in[r]
        sent[r] = dot3(upper, lower, True).reshape(sent.shape[1:])

    if series:
        flag_out[...] = jnp.broadcast_to(worst, flag_out.shape)
        flags[wide] = flag_out[...]
        copies = [
            send(flag_out, flags.at[wide], flag_send.at[k], flag_recv.at[k], wide_peer(k)) for k in range(1, n_wide)
        ]
        for copy in copies:
            copy.wait_recv()
        flag_ref[...] = jnp.max(flags[...], axis=0)
    else:
        flag_ref[...] = jnp.zeros_like(flag_ref)
    last.wait_recv()
    out_ref[:, BLOCK:] = last_in[...]
    for copy in sends:
        copy.wait_send()


def run(columns, sizes, series, collective_id):
    n_wide, n_near, n_far = sizes
    rows = columns.shape[0]
    first, later = 3 * BLOCK // n_near, BLOCK // n_near
    count = ROUNDS - 1
    vmem = lambda *shape: pltpu.VMEM(shape, F32)
    sems = pltpu.SemaphoreType.DMA
    peers = max(n_near, n_far)
    return pl.pallas_call(
        functools.partial(kernel, n_wide, n_near, n_far, series),
        out_shape=(
            jax.ShapeDtypeStruct(columns.shape, F32),
            jax.ShapeDtypeStruct((8, BLOCK), F32),
        ),
        in_specs=[pl.BlockSpec(memory_space=pltpu.VMEM)],
        out_specs=(pl.BlockSpec(memory_space=pltpu.VMEM), pl.BlockSpec(memory_space=pltpu.VMEM)),
        scratch_shapes=[
            vmem(n_near, first, BLOCK), vmem(n_near, first, BLOCK), vmem(n_far, first, BLOCK),
            vmem(n_near, first, BLOCK),
            vmem(count, n_near, later, BLOCK), vmem(count, n_near, later, BLOCK), vmem(count, n_far, later, BLOCK),
            vmem(count, n_near, later, BLOCK),
            vmem(count, rows, BLOCK), vmem(count, rows, BLOCK),
            vmem(count, BLOCK, BLOCK), vmem(count, BLOCK, BLOCK),
            vmem(rows, BLOCK), vmem(rows, BLOCK),
            vmem(8, BLOCK), vmem(n_wide, 8, BLOCK), vmem(2, 2 * BLOCK, 2 * BLOCK),
            sems((ROUNDS, 3, peers)), sems((ROUNDS, 3, peers)),
            sems((count, 2)), sems((count, 2)), sems, sems, sems((n_wide,)), sems((n_wide,)),
        ],
        compiler_params=pltpu.CompilerParams(collective_id=collective_id, has_side_effects=True),
        name="jacobi_series" if series else "jacobi_newton",
    )(columns)


def per_device(sizes, columns):
    fast, rest = run(columns, sizes, True, 0)
    return lax.cond(
        jnp.logical_not(rest[0, 0] <= SERIES_TOL),
        lambda x, y: run(x, sizes, False, 1)[0],
        lambda x, y: y,
        columns, fast,
    )


def solution(mesh, n_near=8):
    sizes = (mesh.shape["wide"], n_near, mesh.shape["row"] // n_near)
    return jax.shard_map(
        functools.partial(per_device, sizes),
        mesh=mesh,
        in_specs=(P("row", "wide"),),
        out_specs=P("row", "wide"),
        check_vma=False,
    )
```

```python
import functools

import jax
import jax.numpy as jnp
from jax import lax
from jax.experimental import pallas as pl
from jax.experimental.pallas import tpu as pltpu
from jax.sharding import PartitionSpec as P

ROUNDS = 4
BLOCK = 128
MESH = pl.DeviceIdType.MESH
F32 = jnp.float32
BF16 = jnp.bfloat16
SERIES_TOL = 1e-12
NEWTON_STEPS = 17


def dims(trans_a, trans_b):
    return (((0 if trans_a else 1,), (1 if trans_b else 0,)), ((), ()))


def dot1(a, b, trans_a=False):
    return lax.dot_general(a.astype(BF16), b.astype(BF16), dims(trans_a, False), preferred_element_type=F32)


def split(x):
    high = x.astype(BF16)
    return high, (x - high.astype(F32)).astype(BF16)


def dot3(a, b, trans_a=False):
    a_high, a_low = split(a)
    b_high, b_low = split(b)
    d = functools.partial(lax.dot_general, dimension_numbers=dims(trans_a, False), preferred_element_type=F32)
    return d(a_high, b_high) + (d(a_high, b_low) + d(a_low, b_high))


def dot6(a, b):
    return lax.dot_general(a, b, dims(False, False), precision=lax.Precision.HIGHEST, preferred_element_type=F32)


def iotas(shape):
    return lax.broadcasted_iota(jnp.int32, shape, 0), lax.broadcasted_iota(jnp.int32, shape, 1)


def half_generator(uu, ul, ll):
    rows, cols = iotas((BLOCK, BLOCK))
    eye = rows == cols
    half_sign = jnp.where(rows < cols, 0.5, jnp.where(rows > cols, -0.5, 0.0)).astype(F32)

    def norms(block):
        only = jnp.where(eye, block, 0.0)
        return jnp.sum(only, axis=1, keepdims=True), jnp.sum(only, axis=0, keepdims=True)

    u_col, u_row = norms(uu)
    l_col, l_row = norms(ll)
    a_uu = half_sign * uu / (u_col + u_row + 1e-06)
    a_ll = half_sign * ll / (l_col + l_row + 1e-06)
    a_ul = 0.5 * ul / (u_col + l_row + 1e-06)
    top = jnp.concatenate([a_uu, a_ul], axis=1)
    low = jnp.concatenate([-a_ul.T, a_ll], axis=1)
    return jnp.concatenate([top, low], axis=0)


def series_turn(a):
    a2 = dot3(a, a)
    both = dot1(jnp.concatenate([a, a2], axis=0), a2)
    width = a.shape[0]
    a3, a4 = both[:width], both[width:]
    first = a + a2 + a3
    both = dot1(jnp.concatenate([first, a4], axis=0), a4)
    rest, a8 = both[:width], both[width:]
    turn = 2.0 * (first + (a4 + (rest + a8)))
    return turn, jnp.sum(a8 * a8, keepdims=True) * jnp.sum(a * a, keepdims=True)


def newton_turn(a, scratch):
    width = a.shape[0]
    rows, cols = iotas((width, width))
    eye = (rows == cols).astype(F32)
    a2 = dot6(a, a)
    bound = jnp.max(jnp.sum(jnp.abs(a2), axis=1, keepdims=True), axis=0, keepdims=True)
    scratch[0] = eye - a
    scratch[1] = (eye + a) * (2.0 / (2.0 + bound))

    def step(_, carry):
        x = scratch[1]
        residual = (rows == cols).astype(F32) - dot6(scratch[0], x)
        scratch[1] = x + dot6(x, residual)
        return carry

    lax.fori_loop(0, NEWTON_STEPS, step, 0)
    return 2.0 * (scratch[1] - eye)


def kernel(n_wide, n_near, n_far, series, x_ref, out_ref, flag_ref,
           sent0, near0, far0, whole0, sent, near, far, whole,
           low_out, low_in, gram_out, gram_in, last_out, last_in, flag_out, flags, newton,
           send_sem, recv_sem, shift_send, shift_recv, last_send, last_recv, flag_send, flag_recv):
    wide, row = lax.axis_index("wide"), lax.axis_index("row")
    me_near, me_far = lax.rem(row, n_near), lax.div(row, n_near)

    def near_peer(k):
        other = lax.rem(me_near + k, n_near)
        return other, {"row": me_far * n_near + other}

    def far_peer(k):
        return {"row": lax.rem(me_far + k, n_far) * n_near + me_near}

    def wide_peer(k):
        return {"wide": lax.rem(wide + (k + n_wide), n_wide)}

    barrier = pltpu.get_barrier_semaphore()
    for k in range(1, n_near):
        pl.semaphore_signal(barrier, inc=1, device_id=near_peer(k)[1], device_id_type=MESH)
    for k in range(1, n_far):
        pl.semaphore_signal(barrier, inc=1, device_id=far_peer(k), device_id_type=MESH)
    for k in range(1, n_wide):
        pl.semaphore_signal(barrier, inc=1, device_id=wide_peer(k), device_id_type=MESH)

    sends = []

    def send(src, dst, ssem, rsem, peer):
        copy = pltpu.make_async_remote_copy(
            src_ref=src, dst_ref=dst, send_sem=ssem, recv_sem=rsem, device_id=peer, device_id_type=MESH
        )
        copy.start()
        sends.append(copy)
        return copy

    def reduce_rows(r, out, near_buf, far_buf, whole_buf):
        copies = []
        for k in range(1, n_near):
            other, peer = near_peer(k)
            copies.append(send(out.at[other], near_buf.at[me_near], send_sem.at[r, 0, k], recv_sem.at[r, 0, k], peer))
        near_buf[me_near] = out[me_near]
        for copy in copies:
            copy.wait_recv()
        total = near_buf[0]
        for i in range(1, n_near):
            total = total + near_buf[i]
        far_buf[me_far] = total
        copies = [
            send(far_buf.at[me_far], far_buf.at[me_far], send_sem.at[r, 1, k], recv_sem.at[r, 1, k], far_peer(k))
            for k in range(1, n_far)
        ]
        for copy in copies:
            copy.wait_recv()
        total = far_buf[0]
        for i in range(1, n_far):
            total = total + far_buf[i]
        whole_buf[me_near] = total
        copies = [
            send(whole_buf.at[me_near], whole_buf.at[me_near], send_sem.at[r, 2, k], recv_sem.at[r, 2, k],
                 near_peer(k)[1])
            for k in range(1, n_near)
        ]
        return copies

    upper, lower = x_ref[:, :BLOCK], x_ref[:, BLOCK:]
    local = dot3(jnp.concatenate([upper, lower], axis=1), jnp.concatenate([upper, lower], axis=1), True)
    payload = jnp.concatenate([local[:BLOCK, BLOCK:], local[:BLOCK, :BLOCK], local[BLOCK:, BLOCK:]], axis=0)
    sent0[...] = payload.reshape(sent0.shape)
    pl.semaphore_wait(barrier, (n_near - 1) + (n_far - 1) + (n_wide - 1))

    worst = jnp.zeros((1, 1), F32)
    for r in range(ROUNDS):
        if r == 0:
            copies = reduce_rows(0, sent0, near0, far0, whole0)
            for copy in copies:
                copy.wait_recv()
            gram = whole0[...].reshape(3 * BLOCK, BLOCK)
            ul, uu, ll = gram[:BLOCK], gram[BLOCK:2 * BLOCK], gram[2 * BLOCK:]
        else:
            copies = reduce_rows(r, sent.at[r - 1], near.at[r - 1], far.at[r - 1], whole.at[r - 1])
            for copy in copies:
                copy.wait_recv()
            gram_copy.wait_recv()
            ul = whole[r - 1].reshape(BLOCK, BLOCK)
            uu, ll = kept_uu, gram_in[r - 1]
        a = half_generator(uu, ul, ll)
        if series:
            turn, rest = series_turn(a)
            worst = jnp.maximum(worst, rest)
        else:
            turn = newton_turn(a, newton)
        pair = jnp.concatenate([upper, lower], axis=1)
        turned = pair + dot3(pair, turn)
        upper = turned[:, :BLOCK]
        if r == ROUNDS - 1:
            last_out[...] = turned[:, BLOCK:]
            last = send(last_out, last_in, last_send, last_recv, wide_peer(-(ROUNDS - 1)))
            out_ref[:, :BLOCK] = upper
            break
        low_out[r] = turned[:, BLOCK:]
        low_copy = send(low_out.at[r], low_in.at[r], shift_send.at[r, 0], shift_recv.at[r, 0], wide_peer(1))
        full = jnp.concatenate(
            [jnp.concatenate([uu, ul], axis=1), jnp.concatenate([ul.T, ll], axis=1)], axis=0
        )
        half = full + dot3(full, turn)
        left, right = half[:, :BLOCK], half[:, BLOCK:]
        kept_uu = left[:BLOCK] + dot3(turn[:, :BLOCK], left, True)
        gram_out[r] = right[BLOCK:] + dot3(turn[:, BLOCK:], right, True)
        gram_copy = send(gram_out.at[r], gram_in.at[r], shift_send.at[r, 1], shift_recv.at[r, 1], wide_peer(1))
        low_copy.wait_recv()
        lower = low_in[r]
        sent[r] = dot3(upper, lower, True).reshape(sent.shape[1:])

    if series:
        flag_out[...] = jnp.broadcast_to(worst, flag_out.shape)
        flags[wide] = flag_out[...]
        copies = [
            send(flag_out, flags.at[wide], flag_send.at[k], flag_recv.at[k], wide_peer(k)) for k in range(1, n_wide)
        ]
        for copy in copies:
            copy.wait_recv()
        flag_ref[0, 0] = jnp.max(jnp.where(flags[...] <= SERIES_TOL, 0, 1))
    else:
        flag_ref[0, 0] = 0
    last.wait_recv()
    out_ref[:, BLOCK:] = last_in[...]
    for copy in sends:
        copy.wait_send()


def run(columns, sizes, series, collective_id):
    n_wide, n_near, n_far = sizes
    rows = columns.shape[0]
    first, later = 3 * BLOCK // n_near, BLOCK // n_near
    count = ROUNDS - 1
    vmem = lambda *shape: pltpu.VMEM(shape, F32)
    sems = pltpu.SemaphoreType.DMA
    peers = max(n_near, n_far)
    return pl.pallas_call(
        functools.partial(kernel, n_wide, n_near, n_far, series),
        out_shape=(
            jax.ShapeDtypeStruct(columns.shape, F32),
            jax.ShapeDtypeStruct((1, 1), jnp.int32),
        ),
        in_specs=[pl.BlockSpec(memory_space=pltpu.VMEM)],
        out_specs=(pl.BlockSpec(memory_space=pltpu.VMEM), pl.BlockSpec(memory_space=pltpu.SMEM)),
        scratch_shapes=[
            vmem(n_near, first, BLOCK), vmem(n_near, first, BLOCK), vmem(n_far, first, BLOCK),
            vmem(n_near, first, BLOCK),
            vmem(count, n_near, later, BLOCK), vmem(count, n_near, later, BLOCK), vmem(count, n_far, later, BLOCK),
            vmem(count, n_near, later, BLOCK),
            vmem(count, rows, BLOCK), vmem(count, rows, BLOCK),
            vmem(count, BLOCK, BLOCK), vmem(count, BLOCK, BLOCK),
            vmem(rows, BLOCK), vmem(rows, BLOCK),
            vmem(8, BLOCK), vmem(n_wide, 8, BLOCK), vmem(2, 2 * BLOCK, 2 * BLOCK),
            sems((ROUNDS, 3, peers)), sems((ROUNDS, 3, peers)),
            sems((count, 2)), sems((count, 2)), sems, sems, sems((n_wide,)), sems((n_wide,)),
        ],
        compiler_params=pltpu.CompilerParams(collective_id=collective_id, has_side_effects=True),
        name="jacobi_series" if series else "jacobi_newton",
    )(columns)


def per_device(sizes, columns):
    fast, short = run(columns, sizes, True, 0)
    return lax.switch(
        short[0, 0],
        [lambda x, y: y, lambda x, y: run(x, sizes, False, 1)[0]],
        columns, fast,
    )


def solution(mesh, n_near=8):
    sizes = (mesh.shape["wide"], n_near, mesh.shape["row"] // n_near)
    return jax.shard_map(
        functools.partial(per_device, sizes),
        mesh=mesh,
        in_specs=(P("row", "wide"),),
        out_specs=P("row", "wide"),
        check_vma=False,
    )
```

```python
import functools

import jax
import jax.numpy as jnp
from jax import lax
from jax.experimental import pallas as pl
from jax.experimental.pallas import tpu as pltpu
from jax.sharding import PartitionSpec as P

BLOCK = 128
MESH = pl.DeviceIdType.MESH
F32 = jnp.float32
BF16 = jnp.bfloat16
SERIES_TOL = 1e-12
NEWTON_STEPS = 17


def dims(trans_a, trans_b):
    return (((0 if trans_a else 1,), (1 if trans_b else 0,)), ((), ()))


def dot1(a, b, trans_a=False):
    return lax.dot_general(a.astype(BF16), b.astype(BF16), dims(trans_a, False), preferred_element_type=F32)


def split(x):
    high = x.astype(BF16)
    return high, (x - high.astype(F32)).astype(BF16)


def dot3(a, b, trans_a=False):
    a_high, a_low = split(a)
    b_high, b_low = split(b)
    d = functools.partial(lax.dot_general, dimension_numbers=dims(trans_a, False), preferred_element_type=F32)
    return d(a_high, b_high) + (d(a_high, b_low) + d(a_low, b_high))


def dot6(a, b):
    return lax.dot_general(a, b, dims(False, False), precision=lax.Precision.HIGHEST, preferred_element_type=F32)


def iotas(shape):
    return lax.broadcasted_iota(jnp.int32, shape, 0), lax.broadcasted_iota(jnp.int32, shape, 1)


def half_generator(uu, ul, ll):
    rows, cols = iotas((BLOCK, BLOCK))
    eye = rows == cols
    half_sign = jnp.where(rows < cols, 0.5, jnp.where(rows > cols, -0.5, 0.0)).astype(F32)

    def norms(block):
        only = jnp.where(eye, block, 0.0)
        return jnp.sum(only, axis=1, keepdims=True), jnp.sum(only, axis=0, keepdims=True)

    u_col, u_row = norms(uu)
    l_col, l_row = norms(ll)
    a_uu = half_sign * uu / (u_col + u_row + 1e-06)
    a_ll = half_sign * ll / (l_col + l_row + 1e-06)
    a_ul = 0.5 * ul / (u_col + l_row + 1e-06)
    top = jnp.concatenate([a_uu, a_ul], axis=1)
    low = jnp.concatenate([-a_ul.T, a_ll], axis=1)
    return jnp.concatenate([top, low], axis=0)


def series_turn(a):
    a2 = dot3(a, a)
    both = dot1(jnp.concatenate([a, a2], axis=0), a2)
    width = a.shape[0]
    a3, a4 = both[:width], both[width:]
    first = a + a2 + a3
    both = dot1(jnp.concatenate([first, a4], axis=0), a4)
    rest, a8 = both[:width], both[width:]
    turn = 2.0 * (first + (a4 + (rest + a8)))
    return turn, jnp.sum(a8 * a8, keepdims=True) * jnp.sum(a * a, keepdims=True)


def newton_turn(a, scratch):
    width = a.shape[0]
    rows, cols = iotas((width, width))
    eye = (rows == cols).astype(F32)
    a2 = dot6(a, a)
    bound = jnp.max(jnp.sum(jnp.abs(a2), axis=1, keepdims=True), axis=0, keepdims=True)
    scratch[0] = eye - a
    scratch[1] = (eye + a) * (2.0 / (2.0 + bound))

    def step(_, carry):
        x = scratch[1]
        residual = (rows == cols).astype(F32) - dot6(scratch[0], x)
        scratch[1] = x + dot6(x, residual)
        return carry

    lax.fori_loop(0, NEWTON_STEPS, step, 0)
    return 2.0 * (scratch[1] - eye)


def kernel(n_wide, n_near, n_far, series, x_hbm, out_ref, flag_ref, x_ref, *refs):
    (reduces, (next_x, turn_out, turn_in, gram_out, gram_in, up_out, up_in, upgram_out, upgram_in, low_out, low_in,
               last_low_out, last_low_in, last_up_out, last_up_in, flag_out, flags, newton),
     (reduce_send, reduce_recv, move_send, move_recv, flag_send, flag_recv, load_sem)) = (
        [refs[4 * i:4 * i + 4] for i in range(4)], refs[16:34], refs[34:])
    wide, row = lax.axis_index("wide"), lax.axis_index("row")
    me_near, me_far = lax.rem(row, n_near), lax.div(row, n_near)

    def near_peer(k):
        other = lax.rem(me_near + k, n_near)
        return other, {"row": me_far * n_near + other}

    def far_peer(k):
        return {"row": lax.rem(me_far + k, n_far) * n_near + me_near}

    def wide_peer(k):
        return {"wide": lax.rem(wide + (k + n_wide), n_wide)}

    load = pltpu.make_async_copy(x_hbm, x_ref, load_sem)
    load.start()
    barrier = pltpu.get_barrier_semaphore()
    for k in range(1, n_near):
        pl.semaphore_signal(barrier, inc=1, device_id=near_peer(k)[1], device_id_type=MESH)
    for k in range(1, n_wide):
        pl.semaphore_signal(barrier, inc=1, device_id=wide_peer(k), device_id_type=MESH)
    for k in range(1, n_far):
        pl.semaphore_signal(barrier, inc=1, device_id=far_peer(k), device_id_type=MESH)

    sends = []

    def send(src, dst, ssem, rsem, peer):
        copy = pltpu.make_async_remote_copy(
            src_ref=src, dst_ref=dst, send_sem=ssem, recv_sem=rsem, device_id=peer, device_id_type=MESH
        )
        copy.start()
        sends.append(copy)
        return copy

    def move(i, src, dst, by):
        return send(src, dst, move_send.at[i], move_recv.at[i], wide_peer(by))

    def arrived(copies):
        for copy in copies:
            copy.wait_recv()

    def total(buf, count):
        value = buf[0]
        for i in range(1, count):
            value = value + buf[i]
        return value

    def scatter(i, payload):
        out, near, far, whole = reduces[i]
        out[...] = payload.reshape(out.shape)
        copies = []
        for k in range(1, n_near):
            other, peer = near_peer(k)
            copies.append(
                send(out.at[other], near.at[me_near], reduce_send.at[i, 0, k], reduce_recv.at[i, 0, k], peer))
        near[me_near] = out[me_near]
        return copies

    def across(i, copies):
        out, near, far, whole = reduces[i]
        arrived(copies)
        far[me_far] = total(near, n_near)
        return [
            send(far.at[me_far], far.at[me_far], reduce_send.at[i, 1, k], reduce_recv.at[i, 1, k], far_peer(k))
            for k in range(1, n_far)
        ]

    def gather(i, copies):
        out, near, far, whole = reduces[i]
        arrived(copies)
        whole[me_near] = total(far, n_far)
        return [
            send(whole.at[me_near], whole.at[me_near], reduce_send.at[i, 2, k], reduce_recv.at[i, 2, k],
                 near_peer(k)[1])
            for k in range(1, n_near)
        ]

    def reduced(i, copies):
        arrived(copies)
        whole = reduces[i][3]
        return whole[...].reshape(-1, BLOCK)

    def blocks(m):
        return jnp.concatenate([m[:BLOCK, :BLOCK], m[:BLOCK, BLOCK:], m[BLOCK:, :BLOCK], m[BLOCK:, BLOCK:]], axis=0)

    def joined(uu, ul, lu, ll):
        return jnp.concatenate(
            [jnp.concatenate([uu, ul], axis=1), jnp.concatenate([lu, ll], axis=1)], axis=0)

    worst = jnp.zeros((1, 1), F32)

    def turn_of(uu, ul, ll):
        nonlocal worst
        a = half_generator(uu, ul, ll)
        if series:
            turn, rest = series_turn(a)
            worst = jnp.maximum(worst, rest)
        else:
            turn = newton_turn(a, newton)
        return turn

    def first_round(s, pair, uu, ul, ll):
        turn = turn_of(uu, ul, ll)
        turn_out[s] = turn[:, BLOCK:]
        turn_copy = move(2 * s, turn_out.at[s], turn_in.at[s], 1)
        full = joined(uu, ul, ul.T, ll)
        half = full + dot3(full, turn)
        gram_out[s] = half[BLOCK:, BLOCK:] + dot3(turn[:, BLOCK:], half[:, BLOCK:], True)
        gram_copy = move(2 * s + 1, gram_out.at[s], gram_in.at[s], 1)
        next_uu = half[:BLOCK, :BLOCK] + dot3(turn[:, :BLOCK], half[:, :BLOCK], True)
        upper = pair[:, :BLOCK] + dot3(pair, turn[:, :BLOCK])
        return turn[:, :BLOCK], upper, next_uu, turn_copy, gram_copy

    def cross_gram(s, left_turn, cross):
        right_turn = turn_in[s]
        half = cross[:, BLOCK:] + dot3(cross, right_turn)
        return half[:BLOCK] + dot3(left_turn, half, True)

    load.wait()
    pair = x_ref[...]
    local = dot3(pair, pair, True)
    payload = jnp.concatenate([local[:BLOCK, BLOCK:], local[:BLOCK, :BLOCK], local[BLOCK:, BLOCK:]], axis=0)
    pl.semaphore_wait(barrier, (n_near - 1) + (n_far - 1) + (n_wide - 1))
    grams = scatter(0, payload)
    next_copy = move(4, x_ref, next_x, 1)
    grams = across(0, grams)
    next_copy.wait_recv()
    next_pair = next_x[...]
    crosses = scatter(1, blocks(dot3(pair, next_pair, True)))
    grams = gather(0, grams)
    crosses = across(1, crosses)
    gram = reduced(0, grams)
    left_turn, upper, uu, turn_copy, gram_copy = first_round(
        0, pair, gram[BLOCK:2 * BLOCK], gram[:BLOCK], gram[2 * BLOCK:])
    crosses = gather(1, crosses)
    turn_copy.wait_recv()
    right_turn = turn_in[0]
    lower = next_pair[:, BLOCK:] + dot3(next_pair, right_turn)
    pair = jnp.concatenate([upper, lower], axis=1)
    gram_copy.wait_recv()
    cross = reduced(1, crosses)
    cross = joined(cross[:BLOCK], cross[BLOCK:2 * BLOCK], cross[2 * BLOCK:3 * BLOCK], cross[3 * BLOCK:])
    ul, ll = cross_gram(0, left_turn, cross), gram_in[0]
    turn = turn_of(uu, ul, ll)
    up_out[...] = pair[:, :BLOCK] + dot3(pair, turn[:, :BLOCK])
    up_copy = move(5, up_out, up_in, -1)
    low_out[...] = pair[:, BLOCK:] + dot3(pair, turn[:, BLOCK:])
    low_copy = move(6, low_out, low_in, 1)
    full = joined(uu, ul, ul.T, ll)
    half = full + dot3(full, turn)
    upgram_out[...] = half[:BLOCK, :BLOCK] + dot3(turn[:, :BLOCK], half[:, :BLOCK], True)
    upgram_copy = move(7, upgram_out, upgram_in, -1)
    ll = half[BLOCK:, BLOCK:] + dot3(turn[:, BLOCK:], half[:, BLOCK:], True)

    kept_up, kept_low = up_out[...], low_out[...]
    low_up = dot3(kept_low, kept_up, True)
    up_copy.wait_recv()
    upper = up_in[...]
    grams = scatter(2, dot3(kept_low, upper, True))
    up_up = dot3(upper, kept_up, True)
    low_copy.wait_recv()
    next_low = low_in[...]
    next_pair = jnp.concatenate([kept_up, next_low], axis=1)
    pair = jnp.concatenate([upper, kept_low], axis=1)
    right = dot3(pair, next_low, True)
    crosses = scatter(3, jnp.concatenate([up_up, right[:BLOCK], low_up, right[BLOCK:]], axis=0))
    grams = across(2, grams)
    crosses = across(3, crosses)
    grams = gather(2, grams)
    upgram_copy.wait_recv()
    ul = reduced(2, grams).T
    left_turn, upper, uu, turn_copy, gram_copy = first_round(1, pair, upgram_in[...], ul, ll)
    crosses = gather(3, crosses)
    turn_copy.wait_recv()
    right_turn = turn_in[1]
    lower = next_pair[:, BLOCK:] + dot3(next_pair, right_turn)
    pair = jnp.concatenate([upper, lower], axis=1)
    gram_copy.wait_recv()
    cross = reduced(3, crosses)
    cross = joined(cross[:BLOCK], cross[BLOCK:2 * BLOCK], cross[2 * BLOCK:3 * BLOCK], cross[3 * BLOCK:])
    turn = turn_of(uu, cross_gram(1, left_turn, cross), gram_in[1])
    last_low_out[...] = pair[:, BLOCK:] + dot3(pair, turn[:, BLOCK:])
    last_low = move(8, last_low_out, last_low_in, -2)
    last_up_out[...] = pair[:, :BLOCK] + dot3(pair, turn[:, :BLOCK])
    last_up = move(9, last_up_out, last_up_in, 1)

    if series:
        flag_out[...] = jnp.broadcast_to(worst, flag_out.shape)
        flags[wide] = flag_out[...]
        arrived([
            send(flag_out, flags.at[wide], flag_send.at[k], flag_recv.at[k], wide_peer(k)) for k in range(1, n_wide)
        ])
        flag_ref[0, 0] = jnp.max(jnp.where(flags[...] <= SERIES_TOL, 0, 1))
    else:
        flag_ref[0, 0] = 0
    last_up.wait_recv()
    out_ref[:, :BLOCK] = last_up_in[...]
    last_low.wait_recv()
    out_ref[:, BLOCK:] = last_low_in[...]
    for copy in sends:
        copy.wait_send()


def run(columns, sizes, series, collective_id):
    n_wide, n_near, n_far = sizes
    rows, width = columns.shape
    vmem = lambda *shape: pltpu.VMEM(shape, F32)
    sems = pltpu.SemaphoreType.DMA
    peers = max(n_near, n_far)
    scratch = [vmem(rows, width)]
    for count in (3, 4, 1, 4):
        piece = count * BLOCK // n_near
        scratch += [vmem(n, piece, BLOCK) for n in (n_near, n_near, n_far, n_near)]
    scratch += [
        vmem(rows, width),
        vmem(2, width, BLOCK), vmem(2, width, BLOCK), vmem(2, BLOCK, BLOCK), vmem(2, BLOCK, BLOCK),
        vmem(rows, BLOCK), vmem(rows, BLOCK), vmem(BLOCK, BLOCK), vmem(BLOCK, BLOCK),
        vmem(rows, BLOCK), vmem(rows, BLOCK),
        vmem(rows, BLOCK), vmem(rows, BLOCK), vmem(rows, BLOCK), vmem(rows, BLOCK),
        vmem(8, BLOCK), vmem(n_wide, 8, BLOCK), vmem(2, width, width),
        sems((4, 3, peers)), sems((4, 3, peers)), sems((10,)), sems((10,)), sems((n_wide,)), sems((n_wide,)), sems,
    ]
    return pl.pallas_call(
        functools.partial(kernel, n_wide, n_near, n_far, series),
        out_shape=(
            jax.ShapeDtypeStruct(columns.shape, F32),
            jax.ShapeDtypeStruct((1, 1), jnp.int32),
        ),
        in_specs=[pl.BlockSpec(memory_space=pl.ANY)],
        out_specs=(pl.BlockSpec(memory_space=pltpu.VMEM), pl.BlockSpec(memory_space=pltpu.SMEM)),
        scratch_shapes=scratch,
        compiler_params=pltpu.CompilerParams(collective_id=collective_id, has_side_effects=True),
        name="jacobi_series" if series else "jacobi_newton",
    )(columns)


def per_device(sizes, columns):
    fast, short = run(columns, sizes, True, 0)
    return lax.switch(
        short[0, 0],
        [lambda x, y: y, lambda x, y: run(x, sizes, False, 1)[0]],
        columns, fast,
    )


def solution(mesh, n_near=8):
    sizes = (mesh.shape["wide"], n_near, mesh.shape["row"] // n_near)
    return jax.shard_map(
        functools.partial(per_device, sizes),
        mesh=mesh,
        in_specs=(P("row", "wide"),),
        out_specs=P("row", "wide"),
        check_vma=False,
    )
```

```python
import functools

import jax
import jax.numpy as jnp
from jax import lax
from jax.experimental import pallas as pl
from jax.experimental.pallas import tpu as pltpu
from jax.sharding import PartitionSpec as P

BLOCK = 128
MESH = pl.DeviceIdType.MESH
F32 = jnp.float32
BF16 = jnp.bfloat16
SERIES_TOL = 1e-12
NEWTON_STEPS = 17


def dims(trans_a, trans_b):
    return (((0 if trans_a else 1,), (1 if trans_b else 0,)), ((), ()))


def dot1(a, b, trans_a=False):
    return lax.dot_general(a.astype(BF16), b.astype(BF16), dims(trans_a, False), preferred_element_type=F32)


def split(x):
    high = x.astype(BF16)
    return high, (x - high.astype(F32)).astype(BF16)


def dot3(a, b, trans_a=False):
    a_high, a_low = split(a)
    b_high, b_low = split(b)
    d = functools.partial(lax.dot_general, dimension_numbers=dims(trans_a, False), preferred_element_type=F32)
    return d(a_high, b_high) + (d(a_high, b_low) + d(a_low, b_high))


def dot6(a, b):
    return lax.dot_general(a, b, dims(False, False), precision=lax.Precision.HIGHEST, preferred_element_type=F32)


def iotas(shape):
    return lax.broadcasted_iota(jnp.int32, shape, 0), lax.broadcasted_iota(jnp.int32, shape, 1)


def half_generator(uu, ul, ll):
    rows, cols = iotas((BLOCK, BLOCK))
    eye = rows == cols
    half_sign = jnp.where(rows < cols, 0.5, jnp.where(rows > cols, -0.5, 0.0)).astype(F32)

    def norms(block):
        only = jnp.where(eye, block, 0.0)
        return jnp.sum(only, axis=1, keepdims=True), jnp.sum(only, axis=0, keepdims=True)

    u_col, u_row = norms(uu)
    l_col, l_row = norms(ll)
    a_uu = half_sign * uu / (u_col + u_row + 1e-06)
    a_ll = half_sign * ll / (l_col + l_row + 1e-06)
    a_ul = 0.5 * ul / (u_col + l_row + 1e-06)
    top = jnp.concatenate([a_uu, a_ul], axis=1)
    low = jnp.concatenate([-a_ul.T, a_ll], axis=1)
    return jnp.concatenate([top, low], axis=0)


def series_turn(a):
    a2 = dot3(a, a)
    both = dot1(jnp.concatenate([a, a2], axis=0), a2)
    width = a.shape[0]
    a3, a4 = both[:width], both[width:]
    first = a + a2 + a3
    both = dot1(jnp.concatenate([first, a4], axis=0), a4)
    rest, a8 = both[:width], both[width:]
    turn = 2.0 * (first + (a4 + (rest + a8)))
    return turn, jnp.sum(a8 * a8, keepdims=True) * jnp.sum(a * a, keepdims=True)


def newton_turn(a, scratch):
    width = a.shape[0]
    rows, cols = iotas((width, width))
    eye = (rows == cols).astype(F32)
    a2 = dot6(a, a)
    bound = jnp.max(jnp.sum(jnp.abs(a2), axis=1, keepdims=True), axis=0, keepdims=True)
    scratch[0] = eye - a
    scratch[1] = (eye + a) * (2.0 / (2.0 + bound))

    def step(_, carry):
        x = scratch[1]
        residual = (rows == cols).astype(F32) - dot6(scratch[0], x)
        scratch[1] = x + dot6(x, residual)
        return carry

    lax.fori_loop(0, NEWTON_STEPS, step, 0)
    return 2.0 * (scratch[1] - eye)


def kernel(n_wide, n_near, n_far, series, x_hbm, out_ref, flag_ref, x_ref, *refs):
    (reduces, (next_x, turn_out, turn_in, gram_out, gram_in, lowgram_out, lowgram_in, next_whole, up_out, up_in, upgram_out, upgram_in, low_out, low_in,
               last_low_out, last_low_in, last_up_out, last_up_in, flag_out, flags, newton),
     (reduce_send, reduce_recv, move_send, move_recv, flag_send, flag_recv, next_send, next_recv, load_sem)) = (
        [refs[4 * i:4 * i + 4] for i in range(6)], refs[24:45], refs[45:])
    wide, row = lax.axis_index("wide"), lax.axis_index("row")
    me_near, me_far = lax.rem(row, n_near), lax.div(row, n_near)

    def near_peer(k):
        other = lax.rem(me_near + k, n_near)
        return other, {"row": me_far * n_near + other}

    def far_peer(k):
        return {"row": lax.rem(me_far + k, n_far) * n_near + me_near}

    def wide_peer(k):
        return {"wide": lax.rem(wide + (k + n_wide), n_wide)}

    def next_near(k, by):
        return near_peer(k)[1] | wide_peer(by)

    load = pltpu.make_async_copy(x_hbm, x_ref, load_sem)
    load.start()
    barrier = pltpu.get_barrier_semaphore()
    for k in sorted(range(1, n_far), key=lambda k: abs(2 * k - n_far)):
        pl.semaphore_signal(barrier, inc=1, device_id=far_peer(k), device_id_type=MESH)
    for k in sorted(range(1, n_wide), key=lambda k: abs(2 * k - n_wide)):
        pl.semaphore_signal(barrier, inc=1, device_id=wide_peer(k), device_id_type=MESH)
    for k in range(1, n_near):
        pl.semaphore_signal(barrier, inc=1, device_id=next_near(k, 1), device_id_type=MESH)
        pl.semaphore_signal(barrier, inc=1, device_id=next_near(k, -1), device_id_type=MESH)
    for k in range(1, n_near):
        pl.semaphore_signal(barrier, inc=1, device_id=near_peer(k)[1], device_id_type=MESH)

    sends = []

    def send(src, dst, ssem, rsem, peer):
        copy = pltpu.make_async_remote_copy(
            src_ref=src, dst_ref=dst, send_sem=ssem, recv_sem=rsem, device_id=peer, device_id_type=MESH
        )
        copy.start()
        sends.append(copy)
        return copy

    def move(i, src, dst, by):
        return send(src, dst, move_send.at[i], move_recv.at[i], wide_peer(by))

    def arrived(copies):
        for copy in copies:
            copy.wait_recv()

    def total(buf, count):
        value = buf[0]
        for i in range(1, count):
            value = value + buf[i]
        return value

    def scatter(i, payload):
        out, near, far, whole = reduces[i]
        out[...] = payload.reshape(out.shape)
        copies = []
        for k in range(1, n_near):
            other, peer = near_peer(k)
            copies.append(
                send(out.at[other], near.at[me_near], reduce_send.at[i, 0, k], reduce_recv.at[i, 0, k], peer))
        near[me_near] = out[me_near]
        return copies

    def across(i, copies):
        out, near, far, whole = reduces[i]
        arrived(copies)
        far[me_far] = total(near, n_near)
        return [
            send(far.at[me_far], far.at[me_far], reduce_send.at[i, 1, k], reduce_recv.at[i, 1, k], far_peer(k))
            for k in range(1, n_far)
        ]

    def gather(i, copies):
        out, near, far, whole = reduces[i]
        arrived(copies)
        whole[me_near] = total(far, n_far)
        return [
            send(whole.at[me_near], whole.at[me_near], reduce_send.at[i, 2, k], reduce_recv.at[i, 2, k],
                 near_peer(k)[1])
            for k in range(1, n_near)
        ]

    def reduced(i, copies):
        arrived(copies)
        whole = reduces[i][3]
        return whole[...].reshape(-1, BLOCK)

    def joined(uu, ul, lu, ll):
        return jnp.concatenate(
            [jnp.concatenate([uu, ul], axis=1), jnp.concatenate([lu, ll], axis=1)], axis=0)

    worst = jnp.zeros((1, 1), F32)

    def turn_of(uu, ul, ll):
        nonlocal worst
        a = half_generator(uu, ul, ll)
        if series:
            turn, rest = series_turn(a)
            worst = jnp.maximum(worst, rest)
        else:
            turn = newton_turn(a, newton)
        return turn

    def turned(turn, uu, ul, ll):
        full = joined(uu, ul, ul.T, ll)
        half = full + dot3(full, turn)
        return (half[:BLOCK, :BLOCK] + dot3(turn[:, :BLOCK], half[:, :BLOCK], True),
                half[BLOCK:, BLOCK:] + dot3(turn[:, BLOCK:], half[:, BLOCK:], True))

    def cross_gram(left_turn, right_turn, cross):
        half = cross[1] + (dot3(cross[0], right_turn[:BLOCK]) + dot3(cross[1], right_turn[BLOCK:]))
        return half[:BLOCK] + dot3(left_turn, half, True)

    load.wait()
    pair = x_ref[...]
    local = dot3(pair, pair, True)
    payload = jnp.concatenate([local[:BLOCK, BLOCK:], local[:BLOCK, :BLOCK], local[BLOCK:, BLOCK:]], axis=0)
    pl.semaphore_wait(barrier, 3 * (n_near - 1) + (n_far - 1) + (n_wide - 1))
    next_up = move(4, x_ref.at[:, :BLOCK], next_x.at[0], 1)
    next_low = move(10, x_ref.at[:, BLOCK:], next_x.at[1], 1)
    grams = scatter(0, payload)
    grams = across(0, grams)
    next_up.wait_recv()
    crosses_up = scatter(1, dot3(pair, next_x[0], True))
    next_low.wait_recv()
    crosses_low = scatter(2, dot3(pair, next_x[1], True))
    next_pair = jnp.concatenate([next_x[0], next_x[1]], axis=1)
    crosses_up = across(1, crosses_up)
    grams = gather(0, grams)
    crosses_low = across(2, crosses_low)
    crosses_up = gather(1, crosses_up)
    gram = reduced(0, grams)
    ul, uu, ll = gram[:BLOCK], gram[BLOCK:2 * BLOCK], gram[2 * BLOCK:]
    turn = turn_of(uu, ul, ll)
    turn_out[...] = turn[:, BLOCK:]
    turn_copy = move(0, turn_out, turn_in, 1)
    crosses_low = gather(2, crosses_low)
    uu, gram_out[...] = turned(turn, uu, ul, ll)
    gram_copy = move(1, gram_out, gram_in, 1)
    left_turn = turn[:, :BLOCK]
    upper = pair[:, :BLOCK] + dot3(pair, left_turn)
    turn_copy.wait_recv()
    right_turn = turn_in[...]
    lower = next_pair[:, BLOCK:] + dot3(next_pair, right_turn)
    pair = jnp.concatenate([upper, lower], axis=1)
    gram_copy.wait_recv()
    cross = reduced(1, crosses_up), reduced(2, crosses_low)
    ul, ll = cross_gram(left_turn, right_turn, cross), gram_in[...]
    turn = turn_of(uu, ul, ll)
    up_out[...] = pair[:, :BLOCK] + dot3(pair, turn[:, :BLOCK])
    up_copy = move(5, up_out, up_in, -1)
    low_out[...] = pair[:, BLOCK:] + dot3(pair, turn[:, BLOCK:])
    low_copy = move(6, low_out, low_in, 1)
    upgram_out[...], lowgram_out[...] = turned(turn, uu, ul, ll)
    upgram_copy = move(7, upgram_out, upgram_in, -1)
    lowgram_copy = move(2, lowgram_out, lowgram_in, 1)

    kept_up, kept_low = up_out[...], low_out[...]
    low_up = dot3(kept_low, kept_up, True)
    up_copy.wait_recv()
    upper = up_in[...]
    grams = scatter(3, dot3(kept_low, upper, True))
    crosses_up = scatter(4, jnp.concatenate([dot3(upper, kept_up, True), low_up], axis=0))
    pair = jnp.concatenate([upper, kept_low], axis=1)
    low_copy.wait_recv()
    next_low = low_in[...]
    crosses_low = scatter(5, dot3(pair, next_low, True))
    next_pair = jnp.concatenate([kept_up, next_low], axis=1)
    grams = across(3, grams)
    crosses_up = across(4, crosses_up)
    crosses_low = across(5, crosses_low)
    grams = gather(3, grams)
    next_grams = [
        send(reduces[3][3].at[me_near], next_whole.at[me_near], next_send.at[k], next_recv.at[k], next_near(k, 1))
        for k in range(n_near)
    ]
    crosses_up = gather(4, crosses_up)
    crosses_low = gather(5, crosses_low)
    upgram_copy.wait_recv()
    uu, ul, ll = upgram_in[...], reduced(3, grams).T, lowgram_out[...]
    turn = turn_of(uu, ul, ll)
    left_turn = turn[:, :BLOCK]
    lowgram_copy.wait_recv()
    arrived(next_grams)
    next_uu, next_ul, next_ll = upgram_out[...], next_whole[...].reshape(BLOCK, BLOCK).T, lowgram_in[...]
    next_turn = turn_of(next_uu, next_ul, next_ll)
    right_turn = next_turn[:, BLOCK:]
    upper = pair[:, :BLOCK] + dot3(pair, left_turn)
    lower = next_pair[:, BLOCK:] + dot3(next_pair, right_turn)
    pair = jnp.concatenate([upper, lower], axis=1)
    uu, _ = turned(turn, uu, ul, ll)
    _, ll = turned(next_turn, next_uu, next_ul, next_ll)
    cross = reduced(4, crosses_up), reduced(5, crosses_low)
    turn = turn_of(uu, cross_gram(left_turn, right_turn, cross), ll)
    if series:
        flag_out[...] = jnp.broadcast_to(worst, flag_out.shape)
        flags[wide] = flag_out[...]
        marks = [
            send(flag_out, flags.at[wide], flag_send.at[k], flag_recv.at[k], wide_peer(k)) for k in range(1, n_wide)
        ]
    last_low_out[...] = pair[:, BLOCK:] + dot3(pair, turn[:, BLOCK:])
    last_low = move(8, last_low_out, last_low_in, -2)
    last_up_out[...] = pair[:, :BLOCK] + dot3(pair, turn[:, :BLOCK])
    last_up = move(9, last_up_out, last_up_in, 1)

    if series:
        arrived(marks)
        flag_ref[0, 0] = jnp.max(jnp.where(flags[...] <= SERIES_TOL, 0, 1))
    else:
        flag_ref[0, 0] = 0
    last_up.wait_recv()
    out_ref[:, :BLOCK] = last_up_in[...]
    last_low.wait_recv()
    out_ref[:, BLOCK:] = last_low_in[...]
    for copy in sends:
        copy.wait_send()


def run(columns, sizes, series, collective_id):
    n_wide, n_near, n_far = sizes
    rows, width = columns.shape
    vmem = lambda *shape: pltpu.VMEM(shape, F32)
    sems = pltpu.SemaphoreType.DMA
    peers = max(n_near, n_far)
    scratch = [vmem(rows, width)]
    for count in (3, 2, 2, 1, 2, 2):
        piece = count * BLOCK // n_near
        scratch += [vmem(n, piece, BLOCK) for n in (n_near, n_near, n_far, n_near)]
    scratch += [
        vmem(2, rows, BLOCK),
        vmem(width, BLOCK), vmem(width, BLOCK), vmem(BLOCK, BLOCK), vmem(BLOCK, BLOCK),
        vmem(BLOCK, BLOCK), vmem(BLOCK, BLOCK), vmem(n_near, BLOCK // n_near, BLOCK),
        vmem(rows, BLOCK), vmem(rows, BLOCK), vmem(BLOCK, BLOCK), vmem(BLOCK, BLOCK),
        vmem(rows, BLOCK), vmem(rows, BLOCK),
        vmem(rows, BLOCK), vmem(rows, BLOCK), vmem(rows, BLOCK), vmem(rows, BLOCK),
        vmem(8, BLOCK), vmem(n_wide, 8, BLOCK), vmem(2, width, width),
        sems((6, 3, peers)), sems((6, 3, peers)), sems((11,)), sems((11,)), sems((n_wide,)), sems((n_wide,)), sems((n_near,)), sems((n_near,)), sems,
    ]
    return pl.pallas_call(
        functools.partial(kernel, n_wide, n_near, n_far, series),
        out_shape=(
            jax.ShapeDtypeStruct(columns.shape, F32),
            jax.ShapeDtypeStruct((1, 1), jnp.int32),
        ),
        in_specs=[pl.BlockSpec(memory_space=pl.ANY)],
        out_specs=(pl.BlockSpec(memory_space=pltpu.VMEM), pl.BlockSpec(memory_space=pltpu.SMEM)),
        scratch_shapes=scratch,
        compiler_params=pltpu.CompilerParams(collective_id=collective_id, has_side_effects=True),
        name="jacobi_series" if series else "jacobi_newton",
    )(columns)


def per_device(sizes, columns):
    fast, short = run(columns, sizes, True, 0)
    return lax.switch(
        short[0, 0],
        [lambda x, y: y, lambda x, y: run(x, sizes, False, 1)[0]],
        columns, fast,
    )


def solution(mesh, n_near=8):
    sizes = (mesh.shape["wide"], n_near, mesh.shape["row"] // n_near)
    return jax.shard_map(
        functools.partial(per_device, sizes),
        mesh=mesh,
        in_specs=(P("row", "wide"),),
        out_specs=P("row", "wide"),
        check_vma=False,
    )
```

```python
import functools

import jax
import jax.numpy as jnp
from jax import lax
from jax.experimental import pallas as pl
from jax.experimental.pallas import tpu as pltpu
from jax.sharding import PartitionSpec as P

BLOCK = 128
MESH = pl.DeviceIdType.MESH
F32 = jnp.float32
BF16 = jnp.bfloat16
SERIES_TOL = 1e-12
NEWTON_STEPS = 17


def dims(trans_a, trans_b):
    return (((0 if trans_a else 1,), (1 if trans_b else 0,)), ((), ()))


def dot1(a, b, trans_a=False):
    return lax.dot_general(a.astype(BF16), b.astype(BF16), dims(trans_a, False), preferred_element_type=F32)


def split(x):
    high = x.astype(BF16)
    return high, (x - high.astype(F32)).astype(BF16)


def dot3(a, b, trans_a=False):
    a_high, a_low = split(a)
    b_high, b_low = split(b)
    d = functools.partial(lax.dot_general, dimension_numbers=dims(trans_a, False), preferred_element_type=F32)
    return d(a_high, b_high) + (d(a_high, b_low) + d(a_low, b_high))


def dot6(a, b):
    return lax.dot_general(a, b, dims(False, False), precision=lax.Precision.HIGHEST, preferred_element_type=F32)


def far_first(count):
    return sorted(range(1, count), key=lambda k: abs(2 * k - count))


def iotas(shape):
    return lax.broadcasted_iota(jnp.int32, shape, 0), lax.broadcasted_iota(jnp.int32, shape, 1)


def half_generator(uu, ul, ll):
    rows, cols = iotas((BLOCK, BLOCK))
    eye = rows == cols
    half_sign = jnp.where(rows < cols, 0.5, jnp.where(rows > cols, -0.5, 0.0)).astype(F32)

    def norms(block):
        only = jnp.where(eye, block, 0.0)
        return jnp.sum(only, axis=1, keepdims=True), jnp.sum(only, axis=0, keepdims=True)

    u_col, u_row = norms(uu)
    l_col, l_row = norms(ll)
    a_uu = half_sign * uu / (u_col + u_row + 1e-06)
    a_ll = half_sign * ll / (l_col + l_row + 1e-06)
    a_ul = 0.5 * ul / (u_col + l_row + 1e-06)
    top = jnp.concatenate([a_uu, a_ul], axis=1)
    low = jnp.concatenate([-a_ul.T, a_ll], axis=1)
    return jnp.concatenate([top, low], axis=0)


def series_turn(a):
    a2 = dot3(a, a)
    both = dot1(jnp.concatenate([a, a2], axis=0), a2)
    width = a.shape[0]
    a3, a4 = both[:width], both[width:]
    first = a + a2 + a3
    both = dot1(jnp.concatenate([first, a4], axis=0), a4)
    rest, a8 = both[:width], both[width:]
    turn = 2.0 * (first + (a4 + (rest + a8)))
    return turn, jnp.sum(a8 * a8, keepdims=True) * jnp.sum(a * a, keepdims=True)


def newton_turn(a, scratch):
    width = a.shape[0]
    rows, cols = iotas((width, width))
    eye = (rows == cols).astype(F32)
    a2 = dot6(a, a)
    bound = jnp.max(jnp.sum(jnp.abs(a2), axis=1, keepdims=True), axis=0, keepdims=True)
    scratch[0] = eye - a
    scratch[1] = (eye + a) * (2.0 / (2.0 + bound))

    def step(_, carry):
        x = scratch[1]
        residual = (rows == cols).astype(F32) - dot6(scratch[0], x)
        scratch[1] = x + dot6(x, residual)
        return carry

    lax.fori_loop(0, NEWTON_STEPS, step, 0)
    return 2.0 * (scratch[1] - eye)


def kernel(n_wide, n_near, n_far, series, x_hbm, out_ref, flag_ref, x_ref, *refs):
    (reduces, (next_x, turn_out, turn_in, gram_out, gram_in, lowgram_out, lowgram_in, next_whole, up_out, up_in, upgram_out, upgram_in, low_out, low_in,
               last_low_out, last_low_in, last_up_out, last_up_in, flag_out, flags, newton),
     (reduce_send, reduce_recv, move_send, move_recv, flag_send, flag_recv, next_send, next_recv, load_sem)) = (
        [refs[4 * i:4 * i + 4] for i in range(6)], refs[24:45], refs[45:])
    wide, row = lax.axis_index("wide"), lax.axis_index("row")
    me_near, me_far = lax.rem(row, n_near), lax.div(row, n_near)

    def near_peer(k):
        other = lax.rem(me_near + k, n_near)
        return other, {"row": me_far * n_near + other}

    def far_peer(k):
        return {"row": lax.rem(me_far + k, n_far) * n_near + me_near}

    def wide_peer(k):
        return {"wide": lax.rem(wide + (k + n_wide), n_wide)}

    def next_near(k, by):
        return near_peer(k)[1] | wide_peer(by)

    load = pltpu.make_async_copy(x_hbm, x_ref, load_sem)
    load.start()
    barrier = pltpu.get_barrier_semaphore()
    for k in sorted(range(1, n_far), key=lambda k: abs(2 * k - n_far)):
        pl.semaphore_signal(barrier, inc=1, device_id=far_peer(k), device_id_type=MESH)
    for k in sorted(range(1, n_wide), key=lambda k: abs(2 * k - n_wide)):
        pl.semaphore_signal(barrier, inc=1, device_id=wide_peer(k), device_id_type=MESH)
    for k in range(1, n_near):
        pl.semaphore_signal(barrier, inc=1, device_id=next_near(k, 1), device_id_type=MESH)
        pl.semaphore_signal(barrier, inc=1, device_id=next_near(k, -1), device_id_type=MESH)
    for k in range(1, n_near):
        pl.semaphore_signal(barrier, inc=1, device_id=near_peer(k)[1], device_id_type=MESH)

    sends = []

    def send(src, dst, ssem, rsem, peer):
        copy = pltpu.make_async_remote_copy(
            src_ref=src, dst_ref=dst, send_sem=ssem, recv_sem=rsem, device_id=peer, device_id_type=MESH
        )
        copy.start()
        sends.append(copy)
        return copy

    def move(i, src, dst, by):
        return send(src, dst, move_send.at[i], move_recv.at[i], wide_peer(by))

    def arrived(copies):
        for copy in copies:
            copy.wait_recv()

    def total(buf, count):
        value = buf[0]
        for i in range(1, count):
            value = value + buf[i]
        return value

    def scatter(i, payload):
        out, near, far, whole = reduces[i]
        out[...] = payload.reshape(out.shape)
        copies = []
        for k in far_first(n_near):
            other, peer = near_peer(k)
            copies.append(
                send(out.at[other], near.at[me_near], reduce_send.at[i, 0, k], reduce_recv.at[i, 0, k], peer))
        near[me_near] = out[me_near]
        return copies

    def across(i, copies):
        out, near, far, whole = reduces[i]
        arrived(copies)
        far[me_far] = total(near, n_near)
        return [
            send(far.at[me_far], far.at[me_far], reduce_send.at[i, 1, k], reduce_recv.at[i, 1, k], far_peer(k))
            for k in range(1, n_far)
        ]

    def gather(i, copies):
        out, near, far, whole = reduces[i]
        arrived(copies)
        whole[me_near] = total(far, n_far)
        return [
            send(whole.at[me_near], whole.at[me_near], reduce_send.at[i, 2, k], reduce_recv.at[i, 2, k],
                 near_peer(k)[1])
            for k in far_first(n_near)
        ]

    def reduced(i, copies):
        arrived(copies)
        whole = reduces[i][3]
        return whole[...].reshape(-1, BLOCK)

    def joined(uu, ul, lu, ll):
        return jnp.concatenate(
            [jnp.concatenate([uu, ul], axis=1), jnp.concatenate([lu, ll], axis=1)], axis=0)

    worst = jnp.zeros((1, 1), F32)

    def turn_of(uu, ul, ll):
        nonlocal worst
        a = half_generator(uu, ul, ll)
        if series:
            turn, rest = series_turn(a)
            worst = jnp.maximum(worst, rest)
        else:
            turn = newton_turn(a, newton)
        return turn

    def turned(turn, uu, ul, ll):
        full = joined(uu, ul, ul.T, ll)
        half = full + dot3(full, turn)
        return (half[:BLOCK, :BLOCK] + dot3(turn[:, :BLOCK], half[:, :BLOCK], True),
                half[BLOCK:, BLOCK:] + dot3(turn[:, BLOCK:], half[:, BLOCK:], True))

    def cross_gram(left_turn, right_turn, cross):
        half = cross[1] + (dot3(cross[0], right_turn[:BLOCK]) + dot3(cross[1], right_turn[BLOCK:]))
        return half[:BLOCK] + dot3(left_turn, half, True)

    load.wait()
    pair = x_ref[...]
    local = dot3(pair, pair, True)
    payload = jnp.concatenate([local[:BLOCK, BLOCK:], local[:BLOCK, :BLOCK], local[BLOCK:, BLOCK:]], axis=0)
    pl.semaphore_wait(barrier, 3 * (n_near - 1) + (n_far - 1) + (n_wide - 1))
    next_up = move(4, x_ref.at[:, :BLOCK], next_x.at[0], 1)
    next_low = move(10, x_ref.at[:, BLOCK:], next_x.at[1], 1)
    grams = scatter(0, payload)
    grams = across(0, grams)
    next_up.wait_recv()
    crosses_up = scatter(1, dot3(pair, next_x[0], True))
    next_low.wait_recv()
    crosses_low = scatter(2, dot3(pair, next_x[1], True))
    next_pair = jnp.concatenate([next_x[0], next_x[1]], axis=1)
    crosses_up = across(1, crosses_up)
    grams = gather(0, grams)
    crosses_low = across(2, crosses_low)
    crosses_up = gather(1, crosses_up)
    gram = reduced(0, grams)
    ul, uu, ll = gram[:BLOCK], gram[BLOCK:2 * BLOCK], gram[2 * BLOCK:]
    turn = turn_of(uu, ul, ll)
    turn_out[...] = turn[:, BLOCK:]
    turn_copy = move(0, turn_out, turn_in, 1)
    crosses_low = gather(2, crosses_low)
    uu, gram_out[...] = turned(turn, uu, ul, ll)
    gram_copy = move(1, gram_out, gram_in, 1)
    left_turn = turn[:, :BLOCK]
    upper = pair[:, :BLOCK] + dot3(pair, left_turn)
    turn_copy.wait_recv()
    right_turn = turn_in[...]
    lower = next_pair[:, BLOCK:] + dot3(next_pair, right_turn)
    pair = jnp.concatenate([upper, lower], axis=1)
    gram_copy.wait_recv()
    cross = reduced(1, crosses_up), reduced(2, crosses_low)
    ul, ll = cross_gram(left_turn, right_turn, cross), gram_in[...]
    turn = turn_of(uu, ul, ll)
    up_out[...] = pair[:, :BLOCK] + dot3(pair, turn[:, :BLOCK])
    up_copy = move(5, up_out, up_in, -1)
    low_out[...] = pair[:, BLOCK:] + dot3(pair, turn[:, BLOCK:])
    low_copy = move(6, low_out, low_in, 1)
    upgram_out[...], lowgram_out[...] = turned(turn, uu, ul, ll)
    upgram_copy = move(7, upgram_out, upgram_in, -1)
    lowgram_copy = move(2, lowgram_out, lowgram_in, 1)

    kept_up, kept_low = up_out[...], low_out[...]
    low_up = dot3(kept_low, kept_up, True)
    up_copy.wait_recv()
    upper = up_in[...]
    grams = scatter(3, dot3(kept_low, upper, True))
    crosses_up = scatter(4, jnp.concatenate([dot3(upper, kept_up, True), low_up], axis=0))
    pair = jnp.concatenate([upper, kept_low], axis=1)
    low_copy.wait_recv()
    next_low = low_in[...]
    crosses_low = scatter(5, dot3(pair, next_low, True))
    next_pair = jnp.concatenate([kept_up, next_low], axis=1)
    grams = across(3, grams)
    crosses_up = across(4, crosses_up)
    crosses_low = across(5, crosses_low)
    grams = gather(3, grams)
    next_grams = [
        send(reduces[3][3].at[me_near], next_whole.at[me_near], next_send.at[k], next_recv.at[k], next_near(k, 1))
        for k in range(n_near)
    ]
    crosses_up = gather(4, crosses_up)
    crosses_low = gather(5, crosses_low)
    upgram_copy.wait_recv()
    uu, ul, ll = upgram_in[...], reduced(3, grams).T, lowgram_out[...]
    turn = turn_of(uu, ul, ll)
    left_turn = turn[:, :BLOCK]
    lowgram_copy.wait_recv()
    arrived(next_grams)
    next_uu, next_ul, next_ll = upgram_out[...], next_whole[...].reshape(BLOCK, BLOCK).T, lowgram_in[...]
    next_turn = turn_of(next_uu, next_ul, next_ll)
    right_turn = next_turn[:, BLOCK:]
    upper = pair[:, :BLOCK] + dot3(pair, left_turn)
    lower = next_pair[:, BLOCK:] + dot3(next_pair, right_turn)
    pair = jnp.concatenate([upper, lower], axis=1)
    uu, _ = turned(turn, uu, ul, ll)
    _, ll = turned(next_turn, next_uu, next_ul, next_ll)
    cross = reduced(4, crosses_up), reduced(5, crosses_low)
    turn = turn_of(uu, cross_gram(left_turn, right_turn, cross), ll)
    if series:
        flag_out[...] = jnp.broadcast_to(worst, flag_out.shape)
        flags[wide] = flag_out[...]
        marks = [
            send(flag_out, flags.at[wide], flag_send.at[k], flag_recv.at[k], wide_peer(k)) for k in range(1, n_wide)
        ]
    half = pair.shape[0] // 2
    last_low_out[:half] = pair[:half, BLOCK:] + dot3(pair[:half], turn[:, BLOCK:])
    last_low = move(8, last_low_out.at[:half], last_low_in.at[:half], -2)
    last_low_out[half:] = pair[half:, BLOCK:] + dot3(pair[half:], turn[:, BLOCK:])
    last_low2 = move(3, last_low_out.at[half:], last_low_in.at[half:], -2)
    last_up_out[...] = pair[:, :BLOCK] + dot3(pair, turn[:, :BLOCK])
    last_up = move(9, last_up_out, last_up_in, 1)

    if series:
        arrived(marks)
        flag_ref[0, 0] = jnp.max(jnp.where(flags[...] <= SERIES_TOL, 0, 1))
    else:
        flag_ref[0, 0] = 0
    last_up.wait_recv()
    out_ref[:, :BLOCK] = last_up_in[...]
    last_low.wait_recv()
    last_low2.wait_recv()
    out_ref[:, BLOCK:] = last_low_in[...]
    for copy in sends:
        copy.wait_send()


def run(columns, sizes, series, collective_id):
    n_wide, n_near, n_far = sizes
    rows, width = columns.shape
    vmem = lambda *shape: pltpu.VMEM(shape, F32)
    sems = pltpu.SemaphoreType.DMA
    peers = max(n_near, n_far)
    scratch = [vmem(rows, width)]
    for count in (3, 2, 2, 1, 2, 2):
        piece = count * BLOCK // n_near
        scratch += [vmem(n, piece, BLOCK) for n in (n_near, n_near, n_far, n_near)]
    scratch += [
        vmem(2, rows, BLOCK),
        vmem(width, BLOCK), vmem(width, BLOCK), vmem(BLOCK, BLOCK), vmem(BLOCK, BLOCK),
        vmem(BLOCK, BLOCK), vmem(BLOCK, BLOCK), vmem(n_near, BLOCK // n_near, BLOCK),
        vmem(rows, BLOCK), vmem(rows, BLOCK), vmem(BLOCK, BLOCK), vmem(BLOCK, BLOCK),
        vmem(rows, BLOCK), vmem(rows, BLOCK),
        vmem(rows, BLOCK), vmem(rows, BLOCK), vmem(rows, BLOCK), vmem(rows, BLOCK),
        vmem(8, BLOCK), vmem(n_wide, 8, BLOCK), vmem(2, width, width),
        sems((6, 3, peers)), sems((6, 3, peers)), sems((11,)), sems((11,)), sems((n_wide,)), sems((n_wide,)), sems((n_near,)), sems((n_near,)), sems,
    ]
    return pl.pallas_call(
        functools.partial(kernel, n_wide, n_near, n_far, series),
        out_shape=(
            jax.ShapeDtypeStruct(columns.shape, F32),
            jax.ShapeDtypeStruct((1, 1), jnp.int32),
        ),
        in_specs=[pl.BlockSpec(memory_space=pl.ANY)],
        out_specs=(pl.BlockSpec(memory_space=pltpu.VMEM), pl.BlockSpec(memory_space=pltpu.SMEM)),
        scratch_shapes=scratch,
        compiler_params=pltpu.CompilerParams(collective_id=collective_id, has_side_effects=True),
        name="jacobi_series" if series else "jacobi_newton",
    )(columns)


def per_device(sizes, columns):
    fast, short = run(columns, sizes, True, 0)
    return lax.switch(
        short[0, 0],
        [lambda x, y: y, lambda x, y: run(x, sizes, False, 1)[0]],
        columns, fast,
    )


def solution(mesh, n_near=8):
    sizes = (mesh.shape["wide"], n_near, mesh.shape["row"] // n_near)
    return jax.shard_map(
        functools.partial(per_device, sizes),
        mesh=mesh,
        in_specs=(P("row", "wide"),),
        out_specs=P("row", "wide"),
        check_vma=False,
    )
```

```python
import functools

import jax
import jax.numpy as jnp
from jax import lax
from jax.experimental import pallas as pl
from jax.experimental.pallas import tpu as pltpu
from jax.sharding import PartitionSpec as P

BLOCK = 128
MESH = pl.DeviceIdType.MESH
F32 = jnp.float32
BF16 = jnp.bfloat16
SERIES_TOL = 1e-12
NEWTON_STEPS = 17


def dims(trans_a, trans_b):
    return (((0 if trans_a else 1,), (1 if trans_b else 0,)), ((), ()))


def dot1(a, b, trans_a=False):
    return lax.dot_general(a.astype(BF16), b.astype(BF16), dims(trans_a, False), preferred_element_type=F32)


def split(x):
    high = x.astype(BF16)
    return high, (x - high.astype(F32)).astype(BF16)


def dot3(a, b, trans_a=False):
    a_high, a_low = split(a)
    b_high, b_low = split(b)
    d = functools.partial(lax.dot_general, dimension_numbers=dims(trans_a, False), preferred_element_type=F32)
    return d(a_high, b_high) + (d(a_high, b_low) + d(a_low, b_high))


def dot6(a, b):
    return lax.dot_general(a, b, dims(False, False), precision=lax.Precision.HIGHEST, preferred_element_type=F32)


def far_first(count):
    return sorted(range(1, count), key=lambda k: abs(2 * k - count))


def iotas(shape):
    return lax.broadcasted_iota(jnp.int32, shape, 0), lax.broadcasted_iota(jnp.int32, shape, 1)


def half_generator(uu, ul, ll):
    rows, cols = iotas((BLOCK, BLOCK))
    eye = rows == cols
    half_sign = jnp.where(rows < cols, 0.5, jnp.where(rows > cols, -0.5, 0.0)).astype(F32)

    def norms(block):
        only = jnp.where(eye, block, 0.0)
        return jnp.sum(only, axis=1, keepdims=True), jnp.sum(only, axis=0, keepdims=True)

    u_col, u_row = norms(uu)
    l_col, l_row = norms(ll)
    a_uu = half_sign * uu / (u_col + u_row + 1e-06)
    a_ll = half_sign * ll / (l_col + l_row + 1e-06)
    a_ul = 0.5 * ul / (u_col + l_row + 1e-06)
    top = jnp.concatenate([a_uu, a_ul], axis=1)
    low = jnp.concatenate([-a_ul.T, a_ll], axis=1)
    return jnp.concatenate([top, low], axis=0)


def series_turn(a):
    a2 = dot3(a, a)
    both = dot1(jnp.concatenate([a, a2], axis=0), a2)
    width = a.shape[0]
    a3, a4 = both[:width], both[width:]
    first = a + a2 + a3
    both = dot1(jnp.concatenate([first, a4], axis=0), a4)
    rest, a8 = both[:width], both[width:]
    turn = 2.0 * (first + (a4 + (rest + a8)))
    return turn, jnp.sum(a8 * a8, keepdims=True) * jnp.sum(a * a, keepdims=True)


def newton_turn(a, scratch):
    width = a.shape[0]
    rows, cols = iotas((width, width))
    eye = (rows == cols).astype(F32)
    a2 = dot6(a, a)
    bound = jnp.max(jnp.sum(jnp.abs(a2), axis=1, keepdims=True), axis=0, keepdims=True)
    scratch[0] = eye - a
    scratch[1] = (eye + a) * (2.0 / (2.0 + bound))

    def step(_, carry):
        x = scratch[1]
        residual = (rows == cols).astype(F32) - dot6(scratch[0], x)
        scratch[1] = x + dot6(x, residual)
        return carry

    lax.fori_loop(0, NEWTON_STEPS, step, 0)
    return 2.0 * (scratch[1] - eye)


def kernel(n_wide, n_near, n_far, series, x_hbm, out_ref, flag_ref, x_ref, *refs):
    (reduces, (next_x, turn_out, turn_in, gram_out, gram_in, lowgram_out, lowgram_in, next_whole, up_out, up_in, upgram_out, upgram_in, low_out, low_in,
               last_low_out, last_up_out, flag_out, flags, newton),
     (reduce_send, reduce_recv, move_send, move_recv, flag_send, flag_recv, next_send, next_recv, load_sem)) = (
        [refs[4 * i:4 * i + 4] for i in range(6)], refs[24:43], refs[43:])
    wide, row = lax.axis_index("wide"), lax.axis_index("row")
    me_near, me_far = lax.rem(row, n_near), lax.div(row, n_near)

    def near_peer(k):
        other = lax.rem(me_near + k, n_near)
        return other, {"row": me_far * n_near + other}

    def far_peer(k):
        return {"row": lax.rem(me_far + k, n_far) * n_near + me_near}

    def wide_peer(k):
        return {"wide": lax.rem(wide + (k + n_wide), n_wide)}

    def next_near(k, by):
        return near_peer(k)[1] | wide_peer(by)

    load = pltpu.make_async_copy(x_hbm, x_ref, load_sem)
    load.start()
    barrier = pltpu.get_barrier_semaphore()
    for k in sorted(range(1, n_far), key=lambda k: abs(2 * k - n_far)):
        pl.semaphore_signal(barrier, inc=1, device_id=far_peer(k), device_id_type=MESH)
    for k in sorted(range(1, n_wide), key=lambda k: abs(2 * k - n_wide)):
        pl.semaphore_signal(barrier, inc=1, device_id=wide_peer(k), device_id_type=MESH)
    for k in range(1, n_near):
        pl.semaphore_signal(barrier, inc=1, device_id=next_near(k, 1), device_id_type=MESH)
        pl.semaphore_signal(barrier, inc=1, device_id=next_near(k, -1), device_id_type=MESH)
    for k in range(1, n_near):
        pl.semaphore_signal(barrier, inc=1, device_id=near_peer(k)[1], device_id_type=MESH)

    sends = []

    def send(src, dst, ssem, rsem, peer):
        copy = pltpu.make_async_remote_copy(
            src_ref=src, dst_ref=dst, send_sem=ssem, recv_sem=rsem, device_id=peer, device_id_type=MESH
        )
        copy.start()
        sends.append(copy)
        return copy

    def move(i, src, dst, by):
        return send(src, dst, move_send.at[i], move_recv.at[i], wide_peer(by))

    def arrived(copies):
        for copy in copies:
            copy.wait_recv()

    def total(buf, count):
        value = buf[0]
        for i in range(1, count):
            value = value + buf[i]
        return value

    def scatter(i, payload):
        out, near, far, whole = reduces[i]
        out[...] = payload.reshape(out.shape)
        copies = []
        for k in far_first(n_near):
            other, peer = near_peer(k)
            copies.append(
                send(out.at[other], near.at[me_near], reduce_send.at[i, 0, k], reduce_recv.at[i, 0, k], peer))
        near[me_near] = out[me_near]
        return copies

    def across(i, copies):
        out, near, far, whole = reduces[i]
        arrived(copies)
        far[me_far] = total(near, n_near)
        return [
            send(far.at[me_far], far.at[me_far], reduce_send.at[i, 1, k], reduce_recv.at[i, 1, k], far_peer(k))
            for k in range(1, n_far)
        ]

    def gather(i, copies):
        out, near, far, whole = reduces[i]
        arrived(copies)
        whole[me_near] = total(far, n_far)
        return [
            send(whole.at[me_near], whole.at[me_near], reduce_send.at[i, 2, k], reduce_recv.at[i, 2, k],
                 near_peer(k)[1])
            for k in far_first(n_near)
        ]

    def reduced(i, copies):
        arrived(copies)
        whole = reduces[i][3]
        return whole[...].reshape(-1, BLOCK)

    def joined(uu, ul, lu, ll):
        return jnp.concatenate(
            [jnp.concatenate([uu, ul], axis=1), jnp.concatenate([lu, ll], axis=1)], axis=0)

    worst = jnp.zeros((1, 1), F32)

    def turn_of(uu, ul, ll):
        nonlocal worst
        a = half_generator(uu, ul, ll)
        if series:
            turn, rest = series_turn(a)
            worst = jnp.maximum(worst, rest)
        else:
            turn = newton_turn(a, newton)
        return turn

    def turned(turn, uu, ul, ll):
        full = joined(uu, ul, ul.T, ll)
        half = full + dot3(full, turn)
        return (half[:BLOCK, :BLOCK] + dot3(turn[:, :BLOCK], half[:, :BLOCK], True),
                half[BLOCK:, BLOCK:] + dot3(turn[:, BLOCK:], half[:, BLOCK:], True))

    def cross_gram(left_turn, right_turn, cross):
        half = cross[1] + (dot3(cross[0], right_turn[:BLOCK]) + dot3(cross[1], right_turn[BLOCK:]))
        return half[:BLOCK] + dot3(left_turn, half, True)

    load.wait()
    pair = x_ref[...]
    local = dot3(pair, pair, True)
    payload = jnp.concatenate([local[:BLOCK, BLOCK:], local[:BLOCK, :BLOCK], local[BLOCK:, BLOCK:]], axis=0)
    pl.semaphore_wait(barrier, 3 * (n_near - 1) + (n_far - 1) + (n_wide - 1))
    next_up = move(4, x_ref.at[:, :BLOCK], next_x.at[0], 1)
    next_low = move(10, x_ref.at[:, BLOCK:], next_x.at[1], 1)
    grams = scatter(0, payload)
    grams = across(0, grams)
    next_up.wait_recv()
    crosses_up = scatter(1, dot3(pair, next_x[0], True))
    next_low.wait_recv()
    crosses_low = scatter(2, dot3(pair, next_x[1], True))
    next_pair = jnp.concatenate([next_x[0], next_x[1]], axis=1)
    crosses_up = across(1, crosses_up)
    grams = gather(0, grams)
    crosses_low = across(2, crosses_low)
    crosses_up = gather(1, crosses_up)
    gram = reduced(0, grams)
    ul, uu, ll = gram[:BLOCK], gram[BLOCK:2 * BLOCK], gram[2 * BLOCK:]
    turn = turn_of(uu, ul, ll)
    turn_out[...] = turn[:, BLOCK:]
    turn_copy = move(0, turn_out, turn_in, 1)
    crosses_low = gather(2, crosses_low)
    uu, gram_out[...] = turned(turn, uu, ul, ll)
    gram_copy = move(1, gram_out, gram_in, 1)
    left_turn = turn[:, :BLOCK]
    upper = pair[:, :BLOCK] + dot3(pair, left_turn)
    turn_copy.wait_recv()
    right_turn = turn_in[...]
    lower = next_pair[:, BLOCK:] + dot3(next_pair, right_turn)
    pair = jnp.concatenate([upper, lower], axis=1)
    gram_copy.wait_recv()
    cross = reduced(1, crosses_up), reduced(2, crosses_low)
    ul, ll = cross_gram(left_turn, right_turn, cross), gram_in[...]
    turn = turn_of(uu, ul, ll)
    up_out[...] = pair[:, :BLOCK] + dot3(pair, turn[:, :BLOCK])
    up_copy = move(5, up_out, up_in, -1)
    low_out[...] = pair[:, BLOCK:] + dot3(pair, turn[:, BLOCK:])
    low_copy = move(6, low_out, low_in, 1)

    kept_up, kept_low = up_out[...], low_out[...]
    low_up = dot3(kept_low, kept_up, True)
    up_copy.wait_recv()
    upper = up_in[...]
    grams = scatter(3, dot3(kept_low, upper, True))
    crosses_up = scatter(4, jnp.concatenate([dot3(upper, kept_up, True), low_up], axis=0))
    pair = jnp.concatenate([upper, kept_low], axis=1)
    low_copy.wait_recv()
    next_low = low_in[...]
    crosses_low = scatter(5, dot3(pair, next_low, True))
    upgram_out[...], lowgram_out[...] = turned(turn, uu, ul, ll)
    upgram_copy = move(7, upgram_out, upgram_in, -1)
    lowgram_copy = move(2, lowgram_out, lowgram_in, 1)
    next_pair = jnp.concatenate([kept_up, next_low], axis=1)
    grams = across(3, grams)
    crosses_up = across(4, crosses_up)
    crosses_low = across(5, crosses_low)
    grams = gather(3, grams)
    next_grams = [
        send(reduces[3][3].at[me_near], next_whole.at[me_near], next_send.at[k], next_recv.at[k], next_near(k, 1))
        for k in range(n_near)
    ]
    crosses_up = gather(4, crosses_up)
    crosses_low = gather(5, crosses_low)
    upgram_copy.wait_recv()
    uu, ul, ll = upgram_in[...], reduced(3, grams).T, lowgram_out[...]
    turn = turn_of(uu, ul, ll)
    left_turn = turn[:, :BLOCK]
    lowgram_copy.wait_recv()
    arrived(next_grams)
    next_uu, next_ul, next_ll = upgram_out[...], next_whole[...].reshape(BLOCK, BLOCK).T, lowgram_in[...]
    next_turn = turn_of(next_uu, next_ul, next_ll)
    right_turn = next_turn[:, BLOCK:]
    upper = pair[:, :BLOCK] + dot3(pair, left_turn)
    lower = next_pair[:, BLOCK:] + dot3(next_pair, right_turn)
    pair = jnp.concatenate([upper, lower], axis=1)
    uu, _ = turned(turn, uu, ul, ll)
    _, ll = turned(next_turn, next_uu, next_ul, next_ll)
    cross = reduced(4, crosses_up), reduced(5, crosses_low)
    turn = turn_of(uu, cross_gram(left_turn, right_turn, cross), ll)
    if series:
        flag_out[...] = jnp.broadcast_to(worst, flag_out.shape)
        flags[wide] = flag_out[...]
        marks = [
            send(flag_out, flags.at[wide], flag_send.at[k], flag_recv.at[k], wide_peer(k)) for k in range(1, n_wide)
        ]
    half = pair.shape[0] // 2
    last_low_out[:half] = pair[:half, BLOCK:] + dot3(pair[:half], turn[:, BLOCK:])
    last_low = move(8, last_low_out.at[:half], out_ref.at[:half, BLOCK:], -2)
    last_low_out[half:] = pair[half:, BLOCK:] + dot3(pair[half:], turn[:, BLOCK:])
    last_low2 = move(3, last_low_out.at[half:], out_ref.at[half:, BLOCK:], -2)
    last_up_out[...] = pair[:, :BLOCK] + dot3(pair, turn[:, :BLOCK])
    last_up = move(9, last_up_out, out_ref.at[:, :BLOCK], 1)

    if series:
        arrived(marks)
        flag_ref[0, 0] = jnp.max(jnp.where(flags[...] <= SERIES_TOL, 0, 1))
    else:
        flag_ref[0, 0] = 0
    last_up.wait_recv()
    last_low.wait_recv()
    last_low2.wait_recv()
    for copy in sends:
        copy.wait_send()


def run(columns, sizes, series, collective_id):
    n_wide, n_near, n_far = sizes
    rows, width = columns.shape
    vmem = lambda *shape: pltpu.VMEM(shape, F32)
    sems = pltpu.SemaphoreType.DMA
    peers = max(n_near, n_far)
    scratch = [vmem(rows, width)]
    for count in (3, 2, 2, 1, 2, 2):
        piece = count * BLOCK // n_near
        scratch += [vmem(n, piece, BLOCK) for n in (n_near, n_near, n_far, n_near)]
    scratch += [
        vmem(2, rows, BLOCK),
        vmem(width, BLOCK), vmem(width, BLOCK), vmem(BLOCK, BLOCK), vmem(BLOCK, BLOCK),
        vmem(BLOCK, BLOCK), vmem(BLOCK, BLOCK), vmem(n_near, BLOCK // n_near, BLOCK),
        vmem(rows, BLOCK), vmem(rows, BLOCK), vmem(BLOCK, BLOCK), vmem(BLOCK, BLOCK),
        vmem(rows, BLOCK), vmem(rows, BLOCK),
        vmem(rows, BLOCK), vmem(rows, BLOCK),
        vmem(8, BLOCK), vmem(n_wide, 8, BLOCK), vmem(2, width, width),
        sems((6, 3, peers)), sems((6, 3, peers)), sems((11,)), sems((11,)), sems((n_wide,)), sems((n_wide,)), sems((n_near,)), sems((n_near,)), sems,
    ]
    return pl.pallas_call(
        functools.partial(kernel, n_wide, n_near, n_far, series),
        out_shape=(
            jax.ShapeDtypeStruct(columns.shape, F32),
            jax.ShapeDtypeStruct((1, 1), jnp.int32),
        ),
        in_specs=[pl.BlockSpec(memory_space=pl.ANY)],
        out_specs=(pl.BlockSpec(memory_space=pltpu.VMEM), pl.BlockSpec(memory_space=pltpu.SMEM)),
        scratch_shapes=scratch,
        compiler_params=pltpu.CompilerParams(collective_id=collective_id, has_side_effects=True),
        name="jacobi_series" if series else "jacobi_newton",
    )(columns)


def per_device(sizes, columns):
    fast, short = run(columns, sizes, True, 0)
    return lax.switch(
        short[0, 0],
        [lambda x, y: y, lambda x, y: run(x, sizes, False, 1)[0]],
        columns, fast,
    )


def solution(mesh, n_near=8):
    sizes = (mesh.shape["wide"], n_near, mesh.shape["row"] // n_near)
    return jax.shard_map(
        functools.partial(per_device, sizes),
        mesh=mesh,
        in_specs=(P("row", "wide"),),
        out_specs=P("row", "wide"),
        check_vma=False,
    )
```
